32 devices in a mesh: wide: 8 (over z, x), narrow: 4 (over y, core).
Axes of the slice: x: 2, y: 2, z: 4, core: 2. Of those that a mesh axis runs over, the one named last changes fastest.
Arguments:
- batch: float32 [128, 768], P('wide'), may hold values from -9 to 9
- targets: float32 [128, 512], P(('wide', 'narrow')), may hold values from -6 to 6
- centers: float32 [4096, 768], P(('wide', 'narrow')), may hold values from -9 to 9
- weights: float32 [4096, 512], P(('wide', 'narrow')), may hold values from -6 to 6
Outputs:
- residual: float32 [128, 512], P(('wide', 'narrow'))
- new_weights: float32 [4096, 512], P(('wide', 'narrow'))
The draws below stay inside these ranges and needn't reach their ends.
All inputs are finite; a program needn't handle non-finite values.
Results may differ from the reference program's by a relative error of at most 0.0001.
Values sent between devices are 32-bit elements; how exact they have to be, the bound alone decides.
No kernel may reach another device: no remote copies, remote signals or barrier semaphores. Data moves between devices by JAX's collectives and lax.ppermute only.
A program may use at most 64 MiB of HBM per device.

```python
import jax
import jax.numpy as jnp
from jax import lax

D = 768
C = 512
M_DEV = 128
CENTERS = 4096
ROWS = 128


cluster_count = 16


latent_dims = 8


mean_spread = 1.58


latent_spread = 0.245


noise_spread = 0.5


def shared_layout(key):
    mean_key = jax.random.fold_in(key, 9101)
    map_key = jax.random.fold_in(key, 9102)
    means = jax.random.normal(mean_key, (cluster_count, D), jnp.float32) * mean_spread
    mapping = jax.random.normal(map_key, (latent_dims, D), jnp.float32)
    return (means, mapping)


def place_points(key, salt, count):
    means, mapping = shared_layout(key)
    own_key = jax.random.fold_in(key, salt)
    label_key, latent_key, noise_key = jax.random.split(own_key, 3)
    labels = jax.random.randint(label_key, (count,), 0, cluster_count)
    latent = jax.random.normal(latent_key, (count, latent_dims), jnp.float32) * latent_spread
    noise = jax.random.normal(noise_key, (count, D), jnp.float32) * noise_spread
    points = means[labels] + jnp.dot(latent, mapping) + noise
    return jnp.clip(points, -9.0, 9.0).astype(jnp.float32)


def draw_batch(key, part):
    return place_points(key, 7301, ROWS)


def draw_centers(key, part):
    return place_points(key, 7302, CENTERS)


def steps_of(rng, dims, pieces, least, top_value):
    loudness = 1.0
    for position, shards_of in pieces:
        heights = jax.random.uniform(jax.random.fold_in(jax.random.fold_in(rng, 6), position), (shards_of,), jnp.float32, least / len(pieces), top_value / len(pieces))
        loudness = loudness * jnp.repeat(jnp.exp(heights), dims[position] // shards_of).reshape((-1,) + (1,) * (len(dims) - 1 - position))
    return loudness


def normal_values(stream_key, dims, width, bound, cuts=(), held_as=jnp.bfloat16):
    values = jax.random.normal(stream_key, dims, jnp.float32) * width
    if len(cuts) > 0:
        values = steps_of(stream_key, dims, cuts, -0.22, 0.18) * values
    return jnp.clip(values, min=-bound, max=bound).astype(held_as)


def setup_inputs(seed: int = 0) -> dict:
    seeds = jax.random.split(jax.random.key(seed), 5)
    batch = draw_batch(jax.random.fold_in(seeds[4], 71), 0)
    targets = normal_values(seeds[1], (ROWS, C), 1.0, 6.0, ((0, 32),), jnp.float32)
    centers = draw_centers(jax.random.fold_in(seeds[4], 71), 0)
    weights = normal_values(seeds[3], (CENTERS, C), 1.0, 6.0, ((0, 32),), jnp.float32)
    return dict(batch=batch, targets=targets, centers=centers, weights=weights)


def kernel_block(points, center_rows):
    row_norms = lax.optimization_barrier(jnp.sum(points * points, axis=1))
    center_norms = lax.optimization_barrier(jnp.sum(center_rows * center_rows, axis=1))
    cross = jnp.dot(points, center_rows.T, precision=lax.Precision.HIGHEST, preferred_element_type=jnp.float32)
    return jnp.exp(-(row_norms[:, None] + center_norms[None, :] - 2.0 * cross) / D)

def reference(batch, targets, centers, weights):
    blocks = CENTERS // M_DEV
    center_blocks = centers.reshape(blocks, M_DEV, D)
    weight_blocks = weights.reshape(blocks, M_DEV, C)
    kernel = lax.map(lambda block: kernel_block(batch, block), center_blocks)

    def accumulate(total, pair):
        return (total + jnp.dot(pair[0], pair[1], precision=lax.Precision.HIGHEST, preferred_element_type=jnp.float32), None)
    start_sum = jnp.zeros((ROWS, C), jnp.float32)
    summed, _ = lax.scan(accumulate, start_sum, (kernel, weight_blocks))
    prediction = summed * (8.0 / jnp.sqrt(jnp.float32(CENTERS)))
    residual = prediction - targets

    def update(pair):
        change = jnp.dot(pair[0].T, residual, precision=lax.Precision.HIGHEST, preferred_element_type=jnp.float32)
        return pair[1] - 32.0 / ROWS * change
    new_blocks = lax.map(update, (kernel, weight_blocks))
    return (residual, new_blocks.reshape(CENTERS, C))
```

```python
import math

import jax
import jax.numpy as jnp
from jax import lax
from jax.sharding import PartitionSpec as P

AXES = ("wide", "narrow")
HIGHEST = lax.Precision.HIGHEST


def bits_of(size):
    return tuple(1 << b for b in reversed(range(size.bit_length() - 1)))


def swap(value, total, mask):
    pairs = [(i, i ^ mask) for i in range(total)]
    return lax.ppermute(value, AXES, pairs)


def shards(batch, targets, centers, weights):
    wide = lax.axis_size("wide")
    narrow = lax.axis_size("narrow")
    total = wide * narrow
    features = centers.shape[1]
    own_rows = targets.shape[0]
    outputs = targets.shape[1]
    all_rows = own_rows * total
    pred_scale = 8.0 / math.sqrt(centers.shape[0] * total)
    spot = lax.axis_index("narrow")
    lane, seat = spot % 2, spot // 2
    seats = narrow // 2

    paired = batch.reshape(seats, 2, own_rows, features)
    rows = jnp.where(lane == 0, paired[:, 0], paired[:, 1]).reshape(seats * own_rows, features)
    other_centers = swap(centers, total, 1)
    other_weights = swap(weights, total, 1)

    for bit in bits_of(wide):
        rows = jnp.concatenate([rows, swap(rows, total, bit * narrow)], axis=0)

    row_norms = jnp.sum(rows * rows, axis=1)

    def block(points):
        norms = jnp.sum(points * points, axis=1)
        cross = jnp.dot(rows, points.T, precision=HIGHEST, preferred_element_type=jnp.float32)
        return jnp.exp(-(row_norms[:, None] + norms[None, :] - 2.0 * cross) / features)

    def product(kernel, values):
        return jnp.dot(kernel, values, precision=HIGHEST, preferred_element_type=jnp.float32)

    kernel_own = block(centers)
    kernel_other = block(other_centers)
    kernel_swapped = swap(kernel_other, total, 1)
    value = (product(kernel_own, weights) + product(kernel_other, other_weights)) * pred_scale

    lead = seats * own_rows
    mine = (jnp.arange(lead) // own_rows == seat)[:, None]
    taken = jnp.where(mine, jnp.tile(targets, (seats, 1)), 0.0)
    value = jnp.concatenate([value[:lead] - taken, value[lead:]], axis=0)

    half = value.shape[0] // 2
    value = value[:half] + swap(value[half:], total, narrow)
    for mask in bits_of(narrow)[:-1]:
        value = value + swap(value, total, mask)
    count = wide // 2
    for bit in reversed(bits_of(wide)[:-1]):
        other = swap(value, total, bit * narrow)
        slow = bit // 2
        fast = count // (2 * slow)
        other = other.reshape(slow, 2, fast, lead, outputs)[:, ::-1].reshape(value.shape)
        value = value + other
    residual = lax.dynamic_slice_in_dim(value, seat * own_rows, own_rows, axis=0)
    value = jnp.concatenate([value, swap(value, total, narrow)], axis=0)
    other_value = swap(value, total, 1)

    def turned(kernel, values):
        return lax.dot_general(
            kernel, values, (((0,), (0,)), ((), ())), precision=HIGHEST, preferred_element_type=jnp.float32
        )

    change = turned(kernel_own, value) + turned(kernel_swapped, other_value)
    new_weights = weights - 32.0 / all_rows * change
    return (residual, new_weights)


def solution(mesh):
    return jax.shard_map(
        shards,
        mesh=mesh,
        in_specs=(
            P("wide", None),
            P(("wide", "narrow"), None),
            P(("wide", "narrow"), None),
            P(("wide", "narrow"), None),
        ),
        out_specs=(P(("wide", "narrow"), None), P(("wide", "narrow"), None)),
        check_vma=False,
    )
```

```python
import functools
import math

import jax
import jax.numpy as jnp
from jax import lax
from jax.experimental import pallas as pl
from jax.experimental.pallas import tpu as pltpu
from jax.sharding import PartitionSpec as P

AXES = ("wide", "narrow")
HIGHEST = lax.Precision.HIGHEST


def odd(number):
    return number.bit_count() % 2


def swap(value, total, masks):
    return lax.ppermute(value, AXES, [(i, i ^ masks[odd(i)]) for i in range(total)])


def flipped(value, place, lead):
    if place is None:
        return value
    shape = (-1, 2, lead << place, value.shape[1])
    return value.reshape(shape)[:, ::-1].reshape(value.shape)


def contract(left, right, dims):
    return lax.dot_general(
        left, right, (dims, ((), ())), precision=HIGHEST, preferred_element_type=jnp.float32
    )


def kernel_columns(rows, points, norms):
    row_norms = jnp.sum(rows * rows, axis=1, keepdims=True)
    cross = contract(rows, points, ((1,), (1,)))
    return jnp.exp(-(row_norms + norms - 2.0 * cross) / rows.shape[1])


def early_body(scale, rows, taken, centers, other_centers, weights, other_weights, value, kernel, norms):
    count = centers.shape[0]
    total = None
    for i, (points, gains) in enumerate(((centers, weights), (other_centers, other_weights))):
        squares = points[...] * points[...]
        norm = contract(jnp.ones((8, squares.shape[1]), jnp.float32), squares, ((1,), (1,)))[:1]
        norms[:, i * count : (i + 1) * count] = norm
        block = kernel_columns(rows[...], points[...], norm)
        kernel[:, i * count : (i + 1) * count] = block
        part = contract(block, gains[...], ((1,), (0,)))
        total = part if total is None else total + part
    lead = taken.shape[0]
    value[...] = total * scale
    value[:lead] = value[:lead] - taken[...]


def late_body(
    scale, rows, early, early_kernel, norms, centers, other_centers, weights, other_weights, value, kernel, other_kernel
):
    count = centers.shape[0]
    half = early.shape[0]
    value[:half] = early[...]
    kernel[:half] = early_kernel[:, :count]
    other_kernel[:half] = early_kernel[:, count:]
    own = kernel_columns(rows[...], centers[...], norms[:, :count])
    other = kernel_columns(rows[...], other_centers[...], norms[:, count:])
    kernel[half:] = own
    other_kernel[half:] = other
    value[half:] = (
        contract(own, weights[...], ((1,), (0,))) + contract(other, other_weights[...], ((1,), (0,)))
    ) * scale


def call(body, outs, *operands):
    return pl.pallas_call(
        body,
        out_shape=[jax.ShapeDtypeStruct(shape, jnp.float32) for shape in outs],
        in_specs=[pl.BlockSpec(memory_space=pltpu.VMEM)] * len(operands),
        out_specs=[pl.BlockSpec(memory_space=pltpu.VMEM)] * len(outs),
        compiler_params=pltpu.CompilerParams(vmem_limit_bytes=LIMIT),
    )(*operands)


LIMIT = 24 * 1024 * 1024


def early_half(rows, taken, scale, centers, other_centers, weights, other_weights):
    half, count, width = rows.shape[0], centers.shape[0], weights.shape[1]
    outs = ((half, width), (half, 2 * count), (1, 2 * count))
    return call(
        functools.partial(early_body, scale), outs, rows, taken, centers, other_centers, weights, other_weights
    )


def late_half(rows, early, early_kernel, norms, scale, centers, other_centers, weights, other_weights):
    half, count, width = rows.shape[0], centers.shape[0], weights.shape[1]
    outs = ((2 * half, width), (2 * half, count), (2 * half, count))
    return call(
        functools.partial(late_body, scale),
        outs, rows, early, early_kernel, norms, centers, other_centers, weights, other_weights,
    )


def shards(batch, targets, centers, weights):
    wide = lax.axis_size("wide")
    narrow = lax.axis_size("narrow")
    total = wide * narrow
    features = centers.shape[1]
    own_rows = targets.shape[0]
    own_count = centers.shape[0]
    all_rows = own_rows * total
    pred_scale = 8.0 / math.sqrt(own_count * total)
    spot = lax.axis_index("narrow")
    lane, seat = spot % 2, spot // 2
    seats = narrow // 2
    lead = seats * own_rows
    place = lax.axis_index(AXES)
    parity = sum((place >> b) & 1 for b in range(total.bit_length() - 1)) % 2

    bits = [narrow << b for b in range(wide.bit_length() - 1)]
    first = [bits[0]] + bits[:0:-1]
    second = first[1:] + first[:1]
    spread = list(zip(first, second))
    line = [2 << b for b in range(seats.bit_length() - 1)] + first[1:2] + first[:1] + first[2:]
    other_line = list(line)
    for i in range(0, len(line) - 1, 2):
        other_line[i : i + 2] = line[i + 1], line[i]
    core = (1, 1)

    def across(value, pair):
        return swap(value, total, (pair[0] ^ 1, pair[1] ^ 1))

    def chosen(block, sign):
        pieces = []
        for s in range(seats):
            start = 2 * s * own_rows
            low, high = block[start : start + own_rows], block[start + own_rows : start + 2 * own_rows]
            want = (lane + sign + sum((s ^ seat) >> b & 1 for b in range(seats.bit_length()))) % 2
            pieces.append(jnp.where(want == 0, low, high))
        return jnp.concatenate(pieces, axis=0)

    other_block = across(batch, spread[0])
    other_centers = swap(centers, total, core)
    other_weights = swap(weights, total, core)
    rows = jnp.concatenate([chosen(batch, 0), chosen(other_block, 1)], axis=0)
    for pair in spread[1:-1]:
        rows = jnp.concatenate([rows, across(rows, pair)], axis=0)
    rows, other_centers, other_weights = lax.optimization_barrier((rows, other_centers, other_weights))
    far_rows = across(rows, spread[-1])

    mine = (jnp.arange(lead) // own_rows == seat)[:, None]
    taken = jnp.where(mine, jnp.tile(targets, (seats, 1)), 0.0)
    operands = (centers, other_centers, weights, other_weights)
    early, early_kernel, norms = early_half(rows, taken, pred_scale, *operands)
    value, kernel, other_kernel = late_half(far_rows, early, early_kernel, norms, pred_scale, *operands)
    swapped = swap(other_kernel, total, core)

    for pair in zip(line, other_line):
        got = across(value, pair)
        turns = [order.index(m) if m in order else None for m, order in zip(pair, (first, second))]
        here, there = (flipped(got, turn, lead) for turn in turns)
        value = value + (here if turns[0] == turns[1] else jnp.where(parity == 0, here, there))
    residual = lax.dynamic_slice_in_dim(value, seat * own_rows, own_rows, axis=0)
    partner = swap(value, total, core)

    def change(kernel, values):
        return lax.dot_general(
            kernel, values, (((0,), (0,)), ((), ())), precision=HIGHEST, preferred_element_type=jnp.float32
        )

    rate = 32.0 / all_rows
    new_weights = weights - rate * change(kernel, value) - rate * change(swapped, partner)
    return (residual, new_weights)


def solution(mesh):
    return jax.shard_map(
        shards,
        mesh=mesh,
        in_specs=(
            P("wide", None),
            P(("wide", "narrow"), None),
            P(("wide", "narrow"), None),
            P(("wide", "narrow"), None),
        ),
        out_specs=(P(("wide", "narrow"), None), P(("wide", "narrow"), None)),
        check_vma=False,
    )
```

```python
import functools
import math

import jax
import jax.numpy as jnp
from jax import lax
from jax.experimental import pallas as pl
from jax.experimental.pallas import tpu as pltpu
from jax.sharding import PartitionSpec as P


AXES = ("wide", "narrow")


def odd(number):
    return number.bit_count() % 2


def swap(value, total, masks):
    return lax.ppermute(value, AXES, [(i, i ^ masks[odd(i)]) for i in range(total)])


def flipped(value, place, lead):
    if place is None:
        return value
    shape = (-1, 2, lead << place, value.shape[1])
    return value.reshape(shape)[:, ::-1].reshape(value.shape)


def contract(left, right, dims):
    return lax.dot_general(left, right, (dims, ((), ())), preferred_element_type=jnp.float32)


def parted(value, count):
    parts = []
    for _ in range(count - 1):
        parts.append(value.astype(jnp.bfloat16))
        value = value - parts[-1].astype(jnp.float32)
    return parts + [value.astype(jnp.bfloat16)]


def contract_parts(left, right, dims):
    count, rows = len(left), left[0].shape[0]
    stack = jnp.concatenate(left, axis=0)
    blocks = [contract(stack[: (count - j) * rows], right[j], dims) for j in range(count)]
    total = None
    for place in reversed(range(count)):
        for j in range(place + 1):
            i = place - j
            term = blocks[j][i * rows : (i + 1) * rows]
            total = term if total is None else total + term
    return total


def point_body(centers, *outs):
    spot = centers[...]
    for ref, piece in zip(outs, parted(spot, POINT_PARTS)):
        ref[...] = piece
    outs[-1][...] = jnp.sum(spot * spot, axis=1)[None, :]


def other_body(centers, weights, other_weights, *outs):
    point_body(centers, *outs[: POINT_PARTS + 1])
    gains = parted(weights[...], GAIN_PARTS) + parted(other_weights[...], GAIN_PARTS)
    for ref, piece in zip(outs[POINT_PARTS + 1 :], gains):
        ref[...] = piece


def sum_body(scale, rows, *refs):
    model, rest = refs[: 2 * MODEL], refs[2 * MODEL :]
    value, kernel, other_kernel = rest[-3:]
    both = [jnp.concatenate([a[...], b[...]], axis=0) for a, b in zip(model[: MODEL - 1], model[MODEL:-1])]
    norms = jnp.concatenate([model[MODEL - 1][...], model[-1][...]], axis=1)
    piece = rows[...]
    row_norms = jnp.sum(piece * piece, axis=1, keepdims=True)
    cross = contract_parts(parted(piece, POINT_PARTS), both[:POINT_PARTS], ((1,), (1,)))
    block = jnp.exp(-(row_norms + norms - 2.0 * cross) / piece.shape[1])
    count = kernel.shape[1]
    kernel[...] = block[:, :count]
    other_kernel[...] = block[:, count:]
    value[...] = contract_parts(parted(block, GAIN_PARTS), both[POINT_PARTS:], ((1,), (0,))) * scale
    if len(rest) == 4:
        taken = rest[0]
        lead = taken.shape[0]
        value[:lead] = value[:lead] - taken[...]


def call(body, outs, *operands):
    return pl.pallas_call(
        body,
        out_shape=[jax.ShapeDtypeStruct(shape, dtype) for shape, dtype in outs],
        in_specs=[pl.BlockSpec(memory_space=pltpu.VMEM)] * len(operands),
        out_specs=[pl.BlockSpec(memory_space=pltpu.VMEM)] * len(outs),
        compiler_params=pltpu.CompilerParams(vmem_limit_bytes=LIMIT),
    )(*operands)


LIMIT = 24 * 1024 * 1024
WIDE, NARROW = jnp.float32, jnp.bfloat16


POINT_PARTS, GAIN_PARTS = 3, 2
MODEL = POINT_PARTS + GAIN_PARTS + 1


def point_outs(centers):
    return [(centers.shape, NARROW)] * POINT_PARTS + [((1, centers.shape[0]), WIDE)]


def own_points(centers):
    return call(point_body, point_outs(centers), centers)


def other_parts(centers, weights, other_weights):
    outs = point_outs(centers) + [(weights.shape, NARROW)] * (2 * GAIN_PARTS)
    *others, a, b, c, d = call(other_body, outs, centers, weights, other_weights)
    return others, (a, b), (c, d)


def row_sums(scale, rows, model, *taken):
    count, width = model[POINT_PARTS].shape
    part = rows.shape[0]
    outs = [((part, width), WIDE), ((part, count), WIDE), ((part, count), WIDE)]
    return call(functools.partial(sum_body, scale), outs, rows, *model, *taken)


def turned_body(near, far, swapped, heads, tails):
    kernel = jnp.concatenate([near[...], far[...], swapped[...]], axis=0)
    heads[...], tails[...] = parted(kernel.T, 2)


def turned_parts(near, far, swapped):
    count = near.shape[1]
    shape = (count, near.shape[0] + far.shape[0] + swapped.shape[0])
    return call(turned_body, [(shape, NARROW), (shape, NARROW)], near, far, swapped)


def final_body(rate, heads, tails, weights, *refs):
    values, out, staged, sems = refs[:-3], refs[-3], refs[-2], refs[-1]
    pieces = staged.shape[0]
    size = staged.shape[2]
    copies = []
    for i in range(pieces):
        columns = slice(i * size, (i + 1) * size)
        value = parted(jnp.concatenate([v[:, columns] for v in values], axis=0), 2)
        staged[i] = weights[:, columns] - rate * contract_parts([heads[...], tails[...]], value, ((1,), (0,)))
        copies.append(pltpu.make_async_copy(staged.at[i], out.at[:, columns], sems.at[i]))
        copies[-1].start()
    for copy in copies:
        copy.wait()


def final_update(rate, turned, weights, values):
    count, width = weights.shape
    pieces = max(1, width // PIECE)
    return pl.pallas_call(
        functools.partial(final_body, rate),
        out_shape=jax.ShapeDtypeStruct(weights.shape, jnp.float32),
        in_specs=[pl.BlockSpec(memory_space=pltpu.VMEM)] * (3 + len(values)),
        out_specs=pl.BlockSpec(memory_space=pl.ANY),
        scratch_shapes=[
            pltpu.VMEM((pieces, count, width // pieces), jnp.float32),
            pltpu.SemaphoreType.DMA((pieces,)),
        ],
        compiler_params=pltpu.CompilerParams(vmem_limit_bytes=LIMIT),
    )(*turned, weights, *values)


PIECE = 128


def shards(batch, targets, centers, weights):
    wide = lax.axis_size("wide")
    narrow = lax.axis_size("narrow")
    total = wide * narrow
    own_rows = targets.shape[0]
    own_count = centers.shape[0]
    all_rows = own_rows * total
    pred_scale = 8.0 / math.sqrt(own_count * total)
    spot = lax.axis_index("narrow")
    lane, seat = spot % 2, spot // 2
    seats = narrow // 2
    lead = seats * own_rows
    place = lax.axis_index(AXES)
    parity = sum((place >> b) & 1 for b in range(total.bit_length() - 1)) % 2

    bits = [narrow << b for b in range(wide.bit_length() - 1)]
    first = [bits[0]] + bits[:0:-1]
    second = first[1:] + first[:1]
    spread = list(zip(first, second))
    seat_bits = [2 << b for b in range(seats.bit_length() - 1)]
    line = seat_bits + first[-2::-1]
    other_line = second[:1] + seat_bits + second[1:-1]
    core = (1, 1)

    def across(value, pair):
        return swap(value, total, (pair[0] ^ 1, pair[1] ^ 1))

    def chosen(block, sign):
        pieces = []
        for s in range(seats):
            start = 2 * s * own_rows
            low, high = block[start : start + own_rows], block[start + own_rows : start + 2 * own_rows]
            want = (lane + sign + sum((s ^ seat) >> b & 1 for b in range(seats.bit_length()))) % 2
            pieces.append(jnp.where(want == 0, low, high))
        return jnp.concatenate(pieces, axis=0)

    other_block = across(batch, spread[0])
    other_centers = swap(centers, total, core)
    other_weights = swap(weights, total, core)
    rows = jnp.concatenate([chosen(batch, 0), chosen(other_block, 1)], axis=0)

    mine = (jnp.arange(lead) // own_rows == seat)[:, None]
    taken = jnp.where(mine, jnp.tile(targets, (seats, 1)), 0.0)
    *points, norms = own_points(centers)
    others, gains, other_gains = other_parts(other_centers, weights, other_weights)
    model = [*points, *gains, norms, *others[:-1], *other_gains, others[-1]]
    for pair in spread[1:-2]:
        rows = jnp.concatenate([rows, across(rows, pair)], axis=0)
    near, far = spread[-2:]
    near_rows = across(rows, near)
    far_rows = [across(rows, far)]
    far_rows.append(swap(rows, total, tuple(a ^ b for a, b in zip(near, far))))
    near_rows = jnp.concatenate([rows, near_rows], axis=0)
    early, early_kernel, early_swap = row_sums(pred_scale, near_rows, model, taken)
    far_rows = jnp.concatenate(far_rows, axis=0)
    sent = across(early, spread[-1])
    late, late_kernel, late_swap = row_sums(pred_scale, far_rows, model)
    swapped = swap(jnp.concatenate([early_swap, late_swap], axis=0), total, core)
    value = late + sent

    for pair in zip(line, other_line):
        got = across(value, pair)
        turns = [order.index(m) if m in order else None for m, order in zip(pair, (first, second))]
        here, there = (flipped(got, turn, lead) for turn in turns)
        value = value + (here if turns[0] == turns[1] else jnp.where(parity == 0, here, there))
    near = across(value, spread[-1])
    mate = swap(value, total, core)
    near_mate = swap(near, total, core)
    residual = lax.dynamic_slice_in_dim(near, seat * own_rows, own_rows, axis=0)

    rate = 32.0 / all_rows

    turned = turned_parts(early_kernel, late_kernel, swapped)
    new_weights = final_update(rate, turned, weights, (near, value, near_mate, mate))
    return (residual, new_weights)


def solution(mesh):
    return jax.shard_map(
        shards,
        mesh=mesh,
        in_specs=(
            P("wide", None),
            P(("wide", "narrow"), None),
            P(("wide", "narrow"), None),
            P(("wide", "narrow"), None),
        ),
        out_specs=(P(("wide", "narrow"), None), P(("wide", "narrow"), None)),
        check_vma=False,
    )
```

```python
import functools
import math

import jax
import jax.numpy as jnp
from jax import lax
from jax.experimental import pallas as pl
from jax.experimental.pallas import tpu as pltpu
from jax.sharding import PartitionSpec as P


AXES = ("wide", "narrow")


def odd(number):
    return number.bit_count() % 2


def swap(value, total, masks):
    return lax.ppermute(value, AXES, [(i, i ^ masks[odd(i)]) for i in range(total)])


def flipped(value, place, lead):
    if place is None:
        return value
    shape = (-1, 2, lead << place, value.shape[1])
    return value.reshape(shape)[:, ::-1].reshape(value.shape)


def contract(left, right, dims):
    return lax.dot_general(left, right, (dims, ((), ())), preferred_element_type=jnp.float32)


def parted(value, count):
    parts = []
    for _ in range(count - 1):
        parts.append(value.astype(jnp.bfloat16))
        value = value - parts[-1].astype(jnp.float32)
    return parts + [value.astype(jnp.bfloat16)]


def contract_parts(left, right, dims):
    count, rows = len(left), left[0].shape[0]
    stack = jnp.concatenate(left, axis=0)
    blocks = [contract(stack[: (count - j) * rows], right[j], dims) for j in range(count)]
    total = None
    for place in reversed(range(count)):
        for j in range(place + 1):
            i = place - j
            term = blocks[j][i * rows : (i + 1) * rows]
            total = term if total is None else total + term
    return total


def point_body(centers, *outs):
    spot = centers[...]
    for ref, piece in zip(outs, parted(spot, POINT_PARTS)):
        ref[...] = piece
    outs[-1][...] = jnp.sum(spot * spot, axis=1)[None, :]


def other_body(centers, weights, other_weights, *outs):
    point_body(centers, *outs[: POINT_PARTS + 1])
    gains = parted(weights[...], GAIN_PARTS) + parted(other_weights[...], GAIN_PARTS)
    for ref, piece in zip(outs[POINT_PARTS + 1 :], gains):
        ref[...] = piece


def sum_body(scale, rows, *refs):
    model, rest = refs[: 2 * MODEL], refs[2 * MODEL :]
    value, kernel, other_kernel = rest[-3:]
    both = [jnp.concatenate([a[...], b[...]], axis=0) for a, b in zip(model[: MODEL - 1], model[MODEL:-1])]
    norms = jnp.concatenate([model[MODEL - 1][...], model[-1][...]], axis=1)
    piece = rows[...]
    row_norms = jnp.sum(piece * piece, axis=1, keepdims=True)
    cross = contract_parts(parted(piece, POINT_PARTS), both[:POINT_PARTS], ((1,), (1,)))
    block = jnp.exp(-(row_norms + norms - 2.0 * cross) / piece.shape[1])
    count = kernel.shape[1]
    kernel[...] = block[:, :count]
    other_kernel[...] = block[:, count:]
    value[...] = contract_parts(parted(block, GAIN_PARTS), both[POINT_PARTS:], ((1,), (0,))) * scale
    if len(rest) == 4:
        taken = rest[0]
        lead = taken.shape[0]
        value[:lead] = value[:lead] - taken[...]


def call(body, outs, *operands):
    return pl.pallas_call(
        body,
        out_shape=[jax.ShapeDtypeStruct(shape, dtype) for shape, dtype in outs],
        in_specs=[pl.BlockSpec(memory_space=pltpu.VMEM)] * len(operands),
        out_specs=[pl.BlockSpec(memory_space=pltpu.VMEM)] * len(outs),
        compiler_params=pltpu.CompilerParams(vmem_limit_bytes=LIMIT),
    )(*operands)


LIMIT = 24 * 1024 * 1024
WIDE, NARROW = jnp.float32, jnp.bfloat16


POINT_PARTS, GAIN_PARTS = 3, 2
MODEL = POINT_PARTS + GAIN_PARTS + 1


def point_outs(centers):
    return [(centers.shape, NARROW)] * POINT_PARTS + [((1, centers.shape[0]), WIDE)]


def own_points(centers):
    return call(point_body, point_outs(centers), centers)


def other_parts(centers, weights, other_weights):
    outs = point_outs(centers) + [(weights.shape, NARROW)] * (2 * GAIN_PARTS)
    *others, a, b, c, d = call(other_body, outs, centers, weights, other_weights)
    return others, (a, b), (c, d)


def row_sums(scale, rows, model, *taken):
    count, width = model[POINT_PARTS].shape
    part = rows.shape[0]
    outs = [((part, width), WIDE), ((part, count), WIDE), ((part, count), WIDE)]
    return call(functools.partial(sum_body, scale), outs, rows, *model, *taken)


def turned_body(near, far, swapped, heads, tails):
    kernel = jnp.concatenate([near[...], far[...], swapped[...]], axis=0)
    heads[...], tails[...] = parted(kernel.T, 2)


def turned_parts(near, far, swapped):
    count = near.shape[1]
    shape = (count, near.shape[0] + far.shape[0] + swapped.shape[0])
    return call(turned_body, [(shape, NARROW), (shape, NARROW)], near, far, swapped)


def final_body(rate, heads, tails, weights, *refs):
    values, out, staged, sems = refs[:-3], refs[-3], refs[-2], refs[-1]
    pieces = staged.shape[0]
    size = staged.shape[2]
    copies = []
    for i in range(pieces):
        columns = slice(i * size, (i + 1) * size)
        value = parted(jnp.concatenate([v[:, columns] for v in values], axis=0), 2)
        staged[i] = weights[:, columns] - rate * contract_parts([heads[...], tails[...]], value, ((1,), (0,)))
        copies.append(pltpu.make_async_copy(staged.at[i], out.at[:, columns], sems.at[i]))
        copies[-1].start()
    for copy in copies:
        copy.wait()


def final_update(rate, turned, weights, values):
    count, width = weights.shape
    pieces = max(1, width // PIECE)
    return pl.pallas_call(
        functools.partial(final_body, rate),
        out_shape=jax.ShapeDtypeStruct(weights.shape, jnp.float32),
        in_specs=[pl.BlockSpec(memory_space=pltpu.VMEM)] * (3 + len(values)),
        out_specs=pl.BlockSpec(memory_space=pl.ANY),
        scratch_shapes=[
            pltpu.VMEM((pieces, count, width // pieces), jnp.float32),
            pltpu.SemaphoreType.DMA((pieces,)),
        ],
        compiler_params=pltpu.CompilerParams(vmem_limit_bytes=LIMIT),
    )(*turned, weights, *values)


PIECE = 128


def shards(batch, targets, centers, weights):
    wide = lax.axis_size("wide")
    narrow = lax.axis_size("narrow")
    total = wide * narrow
    own_rows = targets.shape[0]
    own_count = centers.shape[0]
    all_rows = own_rows * total
    pred_scale = 8.0 / math.sqrt(own_count * total)
    spot = lax.axis_index("narrow")
    lane, seat = spot % 2, spot // 2
    seats = narrow // 2
    lead = seats * own_rows
    place = lax.axis_index(AXES)
    parity = sum((place >> b) & 1 for b in range(total.bit_length() - 1)) % 2

    bits = [narrow << b for b in range(wide.bit_length() - 1)]
    first = [bits[0]] + bits[:0:-1]
    second = first[1:] + first[:1]
    spread = list(zip(first, second))
    seat_bits = [2 << b for b in range(seats.bit_length() - 1)]
    line = seat_bits + first[-2::-1]
    other_line = second[:1] + seat_bits + second[1:-1]
    core = (1, 1)

    def across(value, pair):
        return swap(value, total, (pair[0] ^ 1, pair[1] ^ 1))

    def chosen(block, sign):
        pieces = []
        for s in range(seats):
            start = 2 * s * own_rows
            low, high = block[start : start + own_rows], block[start + own_rows : start + 2 * own_rows]
            want = (lane + sign + sum((s ^ seat) >> b & 1 for b in range(seats.bit_length()))) % 2
            pieces.append(jnp.where(want == 0, low, high))
        return jnp.concatenate(pieces, axis=0)

    other_block = across(batch, spread[0])
    other_centers = swap(centers, total, core)
    other_weights = swap(weights, total, core)
    rows = jnp.concatenate([chosen(batch, 0), chosen(other_block, 1)], axis=0)

    mine = (jnp.arange(lead) // own_rows == seat)[:, None]
    taken = jnp.where(mine, jnp.tile(targets, (seats, 1)), 0.0)
    *points, norms = own_points(centers)
    others, gains, other_gains = other_parts(other_centers, weights, other_weights)
    model = [*points, *gains, norms, *others[:-1], *other_gains, others[-1]]
    for pair in spread[1:-2]:
        rows = jnp.concatenate([rows, across(rows, pair)], axis=0)
    near, far = spread[-2:]
    near_rows = across(rows, near)
    far_rows = [across(rows, far)]
    far_rows.append(swap(rows, total, tuple(a ^ b for a, b in zip(near, far))))
    near_rows = jnp.concatenate([rows, near_rows], axis=0)
    early, early_kernel, early_swap = row_sums(pred_scale, near_rows, model, taken)
    far_rows = jnp.concatenate(far_rows, axis=0)
    sent = across(early, spread[-1])
    late, late_kernel, late_swap = row_sums(pred_scale, far_rows, model)
    swapped = swap(jnp.concatenate([early_swap, late_swap], axis=0), total, core)
    turned = turned_parts(early_kernel, late_kernel, swapped)
    value = late + sent

    def turned_rows(got, pair):
        turns = [order.index(m) if m in order else None for m, order in zip(pair, (first, second))]
        here, there = (flipped(got, turn, lead) for turn in turns)
        return here if turns[0] == turns[1] else jnp.where(parity == 0, here, there)

    *inner, last = zip(line, other_line)
    for pair in inner:
        got = across(value, pair)
        value = value + turned_rows(got, pair)
    side = across(value, last)
    corner = swap(value, total, tuple(a ^ b for a, b in zip(last, far)))
    near_sum = across(value, far)
    value = value + turned_rows(side, last)
    near_sum = near_sum + turned_rows(corner, last)
    full = jnp.concatenate([near_sum, value], axis=0)
    partner = swap(full, total, core)
    residual = lax.dynamic_slice_in_dim(near_sum, seat * own_rows, own_rows, axis=0)

    rate = 32.0 / all_rows

    new_weights = final_update(rate, turned, weights, (full, partner))
    return (residual, new_weights)


def solution(mesh):
    return jax.shard_map(
        shards,
        mesh=mesh,
        in_specs=(
            P("wide", None),
            P(("wide", "narrow"), None),
            P(("wide", "narrow"), None),
            P(("wide", "narrow"), None),
        ),
        out_specs=(P(("wide", "narrow"), None), P(("wide", "narrow"), None)),
        check_vma=False,
    )
```

```python
import functools
import math

import jax
import jax.numpy as jnp
from jax import lax
from jax.experimental import pallas as pl
from jax.experimental.pallas import tpu as pltpu
from jax.sharding import PartitionSpec as P


AXES = ("wide", "narrow")


def odd(number):
    return number.bit_count() % 2


def swap(value, total, masks):
    return lax.ppermute(value, AXES, [(i, i ^ masks[odd(i)]) for i in range(total)])


def flipped(value, place, lead):
    if place is None:
        return value
    shape = (-1, 2, lead << place, value.shape[1])
    return value.reshape(shape)[:, ::-1].reshape(value.shape)


def contract(left, right, dims):
    return lax.dot_general(left, right, (dims, ((), ())), preferred_element_type=jnp.float32)


def parted(value, count):
    parts = []
    for _ in range(count - 1):
        parts.append(value.astype(jnp.bfloat16))
        value = value - parts[-1].astype(jnp.float32)
    return parts + [value.astype(jnp.bfloat16)]


def contract_parts(left, right, dims):
    count, rows = len(left), left[0].shape[0]
    stack = jnp.concatenate(left, axis=0)
    blocks = [contract(stack[: (count - j) * rows], right[j], dims) for j in range(count)]
    total = None
    for place in reversed(range(count)):
        for j in range(place + 1):
            i = place - j
            term = blocks[j][i * rows : (i + 1) * rows]
            total = term if total is None else total + term
    return total


def point_body(centers, *outs):
    spot = centers[...]
    for ref, piece in zip(outs, parted(spot, POINT_PARTS)):
        ref[...] = piece
    outs[-1][...] = jnp.sum(spot * spot, axis=1)[None, :]


def other_body(centers, weights, other_weights, *outs):
    point_body(centers, *outs[: POINT_PARTS + 1])
    gains = parted(weights[...], GAIN_PARTS) + parted(other_weights[...], GAIN_PARTS)
    for ref, piece in zip(outs[POINT_PARTS + 1 :], gains):
        ref[...] = piece


def sum_body(scale, rows, *refs):
    model, rest = refs[: 2 * MODEL], refs[2 * MODEL :]
    value, kernel, other_kernel = rest[-3:]
    both = [jnp.concatenate([a[...], b[...]], axis=0) for a, b in zip(model[: MODEL - 1], model[MODEL:-1])]
    norms = jnp.concatenate([model[MODEL - 1][...], model[-1][...]], axis=1)
    piece = rows[...]
    row_norms = jnp.sum(piece * piece, axis=1, keepdims=True)
    cross = contract_parts(parted(piece, POINT_PARTS), both[:POINT_PARTS], ((1,), (1,)))
    block = jnp.exp(-(row_norms + norms - 2.0 * cross) / piece.shape[1])
    count = kernel.shape[1]
    kernel[...] = block[:, :count]
    other_kernel[...] = block[:, count:]
    value[...] = contract_parts(parted(block, GAIN_PARTS), both[POINT_PARTS:], ((1,), (0,))) * scale
    if len(rest) == 4:
        taken = rest[0]
        lead = taken.shape[0]
        value[:lead] = value[:lead] - taken[...]


def call(body, outs, *operands):
    return pl.pallas_call(
        body,
        out_shape=[jax.ShapeDtypeStruct(shape, dtype) for shape, dtype in outs],
        in_specs=[pl.BlockSpec(memory_space=pltpu.VMEM)] * len(operands),
        out_specs=[pl.BlockSpec(memory_space=pltpu.VMEM)] * len(outs),
        compiler_params=pltpu.CompilerParams(vmem_limit_bytes=LIMIT),
    )(*operands)


LIMIT = 24 * 1024 * 1024
WIDE, NARROW = jnp.float32, jnp.bfloat16


POINT_PARTS, GAIN_PARTS = 3, 2
MODEL = POINT_PARTS + GAIN_PARTS + 1


def point_outs(centers):
    return [(centers.shape, NARROW)] * POINT_PARTS + [((1, centers.shape[0]), WIDE)]


def own_points(centers):
    return call(point_body, point_outs(centers), centers)


def other_parts(centers, weights, other_weights):
    outs = point_outs(centers) + [(weights.shape, NARROW)] * (2 * GAIN_PARTS)
    *others, a, b, c, d = call(other_body, outs, centers, weights, other_weights)
    return others, (a, b), (c, d)


def row_sums(scale, rows, model, *taken):
    count, width = model[POINT_PARTS].shape
    part = rows.shape[0]
    outs = [((part, width), WIDE), ((part, count), WIDE), ((part, count), WIDE)]
    return call(functools.partial(sum_body, scale), outs, rows, *model, *taken)


def turned_body(near, far, swapped, *outs):
    own = jnp.concatenate([near[...], far[...]], axis=0)
    for ref, piece in zip(outs, parted(own.T, 2) + parted(swapped[...].T, 2)):
        ref[...] = piece


def turned_parts(near, far, swapped):
    shape = (near.shape[1], swapped.shape[0])
    a, b, c, d = call(turned_body, [(shape, NARROW)] * 4, near, far, swapped)
    return (a, b), (c, d)


def base_body(rate, heads, tails, weights, values, out):
    out[...] = weights[...] - rate * contract_parts([heads[...], tails[...]], parted(values[...], 2), ((1,), (0,)))


def base_update(rate, turned, weights, values):
    return call(functools.partial(base_body, rate), [(weights.shape, WIDE)], *turned, weights, values)[0]


def final_body(rate, heads, tails, weights, *refs):
    values, out, staged, sems = refs[:-3], refs[-3], refs[-2], refs[-1]
    pieces, size = staged.shape[0], staged.shape[1]
    value = parted(jnp.concatenate([v[...] for v in values], axis=0), 2)
    copies = []
    for i in range(pieces):
        part = slice(i * size, (i + 1) * size)
        staged[i] = weights[part] - rate * contract_parts([heads[part], tails[part]], value, ((1,), (0,)))
        copies.append(pltpu.make_async_copy(staged.at[i], out.at[part], sems.at[i]))
        copies[-1].start()
    for copy in copies:
        copy.wait()


def final_update(rate, turned, weights, values):
    count, width = weights.shape
    pieces = max(1, count // PIECE)
    return pl.pallas_call(
        functools.partial(final_body, rate),
        out_shape=jax.ShapeDtypeStruct(weights.shape, jnp.float32),
        in_specs=[pl.BlockSpec(memory_space=pltpu.VMEM)] * (3 + len(values)),
        out_specs=pl.BlockSpec(memory_space=pl.ANY),
        scratch_shapes=[
            pltpu.VMEM((pieces, count // pieces, width), jnp.float32),
            pltpu.SemaphoreType.DMA((pieces,)),
        ],
        compiler_params=pltpu.CompilerParams(vmem_limit_bytes=LIMIT),
    )(*turned, weights, *values)


PIECE = 64


def shards(batch, targets, centers, weights):
    wide = lax.axis_size("wide")
    narrow = lax.axis_size("narrow")
    total = wide * narrow
    own_rows = targets.shape[0]
    own_count = centers.shape[0]
    all_rows = own_rows * total
    pred_scale = 8.0 / math.sqrt(own_count * total)
    spot = lax.axis_index("narrow")
    lane, seat = spot % 2, spot // 2
    seats = narrow // 2
    lead = seats * own_rows
    place = lax.axis_index(AXES)
    parity = sum((place >> b) & 1 for b in range(total.bit_length() - 1)) % 2

    bits = [narrow << b for b in range(wide.bit_length() - 1)]
    first = [bits[0]] + bits[:0:-1]
    second = first[1:] + first[:1]
    spread = list(zip(first, second))
    seat_bits = [2 << b for b in range(seats.bit_length() - 1)]
    line = seat_bits + first[-2::-1]
    other_line = second[:1] + seat_bits + second[1:-1]
    core = (1, 1)

    def across(value, pair):
        return swap(value, total, (pair[0] ^ 1, pair[1] ^ 1))

    def chosen(block, sign):
        pieces = []
        for s in range(seats):
            start = 2 * s * own_rows
            low, high = block[start : start + own_rows], block[start + own_rows : start + 2 * own_rows]
            want = (lane + sign + sum((s ^ seat) >> b & 1 for b in range(seats.bit_length()))) % 2
            pieces.append(jnp.where(want == 0, low, high))
        return jnp.concatenate(pieces, axis=0)

    other_block = across(batch, spread[0])
    other_centers = swap(centers, total, core)
    other_weights = swap(weights, total, core)
    rows = jnp.concatenate([chosen(batch, 0), chosen(other_block, 1)], axis=0)

    mine = (jnp.arange(lead) // own_rows == seat)[:, None]
    taken = jnp.where(mine, jnp.tile(targets, (seats, 1)), 0.0)
    *points, norms = own_points(centers)
    others, gains, other_gains = other_parts(other_centers, weights, other_weights)
    model = [*points, *gains, norms, *others[:-1], *other_gains, others[-1]]
    for pair in spread[1:-2]:
        rows = jnp.concatenate([rows, across(rows, pair)], axis=0)
    near, far = spread[-2:]
    near_rows = across(rows, near)
    far_rows = [across(rows, far)]
    far_rows.append(swap(rows, total, tuple(a ^ b for a, b in zip(near, far))))
    near_rows = jnp.concatenate([rows, near_rows], axis=0)
    early, early_kernel, early_swap = row_sums(pred_scale, near_rows, model, taken)
    far_rows = jnp.concatenate(far_rows, axis=0)
    sent = across(early, spread[-1])
    late, late_kernel, late_swap = row_sums(pred_scale, far_rows, model)
    swapped = swap(jnp.concatenate([early_swap, late_swap], axis=0), total, core)
    turned = turned_parts(early_kernel, late_kernel, swapped)
    value = late + sent

    def turned_rows(got, pair):
        turns = [order.index(m) if m in order else None for m, order in zip(pair, (first, second))]
        here, there = (flipped(got, turn, lead) for turn in turns)
        return here if turns[0] == turns[1] else jnp.where(parity == 0, here, there)

    *inner, last = zip(line, other_line)
    for pair in inner:
        got = across(value, pair)
        value = value + turned_rows(got, pair)
    side = across(value, last)
    corner = swap(value, total, tuple(a ^ b for a, b in zip(last, far)))
    near_sum = across(value, far)
    value = value + turned_rows(side, last)
    near_sum = near_sum + turned_rows(corner, last)
    full = jnp.concatenate([near_sum, value], axis=0)
    partner = swap(full, total, core)
    residual = lax.dynamic_slice_in_dim(near_sum, seat * own_rows, own_rows, axis=0)

    rate = 32.0 / all_rows

    base = base_update(rate, turned[0], weights, full)
    new_weights = final_update(rate, turned[1], base, (partner,))
    return (residual, new_weights)


def solution(mesh):
    return jax.shard_map(
        shards,
        mesh=mesh,
        in_specs=(
            P("wide", None),
            P(("wide", "narrow"), None),
            P(("wide", "narrow"), None),
            P(("wide", "narrow"), None),
        ),
        out_specs=(P(("wide", "narrow"), None), P(("wide", "narrow"), None)),
        check_vma=False,
    )
```
